256 devices in a mesh: tm: 16 (over x_hi, z), row: 8 (over y, core), col: 2 (over x_lo).
Axes of the slice: x: 4 (x_hi: 2, x_lo: 2; x = x_hi * 2 + x_lo), y: 4, z: 8, core: 2. Of those that a mesh axis runs over, the one named last changes fastest.
Arguments:
- frames: float32 [16, 2048, 1024], P('tm', 'row', 'col'), may hold values from 0 to 200, as said below
- following: float32 [2048, 1024], P('row', 'col'), may hold values from 0 to 200, as said below
Outputs:
- planes: float32 [16, 64, 64, 2048], P('tm', 'row', None, 'col')
The draws below stay inside these ranges and needn't reach their ends.
Inputs may be any that keep to these rules, and one draw needn't show every extreme that they name: `frames`: detector intensities, never negative. `following`: detector intensities, never negative.
All inputs are finite; a program needn't handle non-finite values.
Results may differ from the reference program's by a relative error of at most 0.000071.
Values sent between devices are 32-bit elements; how exact they have to be, the bound alone decides.
No kernel may reach another device: no remote copies, remote signals or barrier semaphores. Data moves between devices by JAX's collectives and lax.ppermute only.
A program may use at most 128 MiB of HBM per device.

```python
import math
import jax
import jax.numpy as jnp
from jax import lax

W = 64
STRIDE = 32
FRAMES = 16
NROWS = 2048
NCOLS = 1024


def speckle(key, frame_total):
    grain_key = jax.random.fold_in(key, 0)
    row_key = jax.random.fold_in(key, 2)
    col_key = jax.random.fold_in(key, 3)
    grains = jnp.minimum(jax.random.exponential(grain_key, (frame_total, NROWS, NCOLS), jnp.float32), 12.0)
    log_span = math.log(10.0)
    row_gain = jnp.exp(log_span * jax.random.uniform(row_key, (frame_total, NROWS, 1), jnp.float32))
    col_gain = jnp.exp(log_span * jax.random.uniform(col_key, (frame_total, 1, NCOLS), jnp.float32))
    return grains * row_gain * col_gain / math.exp(log_span)


def draw_frames(key, part):
    return speckle(jax.random.fold_in(key, 11), FRAMES)


def draw_following(key, part):
    return speckle(jax.random.fold_in(key, 23), 1)[0]


def setup_inputs(seed: int = 0) -> dict:
    key_list = jax.random.split(jax.random.key(seed), 3)
    frames = draw_frames(jax.random.fold_in(key_list[2], 71), 0)
    following = draw_following(jax.random.fold_in(key_list[2], 71), 0)
    return dict(frames=frames, following=following)


def cut_windows(frame):
    padded = jnp.pad(frame, ((0, STRIDE), (0, STRIDE)))
    blocks = padded.reshape(NROWS // STRIDE + 1, STRIDE, NCOLS // STRIDE + 1, STRIDE)
    row_pairs = jnp.concatenate([blocks[:-1], blocks[1:]], axis=1)
    windows = jnp.concatenate([row_pairs[:, :, :-1], row_pairs[:, :, 1:]], axis=3)
    centred = windows - lax.optimization_barrier(jnp.mean(windows, axis=(1, 3), keepdims=True))
    spread = lax.optimization_barrier(jnp.mean(centred * centred, axis=(1, 3), keepdims=True))
    return centred * lax.rsqrt(spread + 1e-05)

def pair_planes(pair):
    current, upcoming = pair
    first = jnp.fft.fft2(cut_windows(current), axes=(1, 3))
    second = jnp.fft.fft2(cut_windows(upcoming), axes=(1, 3))
    summed = jnp.real(jnp.fft.ifft2(jnp.conj(first) * second, axes=(1, 3))) / W
    return summed.reshape(NROWS // STRIDE, W, NCOLS // STRIDE * W).astype(jnp.float32)

def reference(frames, following):
    upcoming = jnp.concatenate([frames[1:], following[None]], axis=0)
    return lax.map(pair_planes, (frames, upcoming))
```

```python
import jax
import jax.numpy as jnp
import ml_dtypes
import numpy as np
from jax import lax
from jax.experimental import pallas as pl
from jax.experimental.pallas import tpu as pltpu
from jax.sharding import PartitionSpec as P

W = 64
STRIDE = 32
HALF = W // 2
LANES = 128
EPS = 1e-05
F32 = jnp.float32
BF16 = jnp.bfloat16


def parts_of(table, count):
    rest = np.asarray(table, np.float64)
    out = []
    for _ in range(count):
        part = rest.astype(ml_dtypes.bfloat16)
        out.append(part)
        rest = rest - part.astype(np.float64)
    return out


def two_windows(block):
    zero = np.zeros_like(block)
    return np.block([[block, zero], [zero, block]])


def make_tables():
    index = np.arange(W)
    turns = 2.0 * np.pi / W * (index[:, None] * index[None, :] % W)
    cosine, sine = np.cos(turns), np.sin(turns)
    slots = np.arange(HALF)
    down = np.concatenate([cosine[:HALF], -sine[:HALF]], axis=0)
    down[0] = 0.0
    down[HALF] = cosine[HALF]
    hi, lo = parts_of(down, 2)
    down_table = np.concatenate([hi, hi, lo], axis=1)
    across = np.concatenate([two_windows(cosine), two_windows(sine)], axis=1)
    hi, lo, low = parts_of(across, 3)
    across_table = np.concatenate([hi, hi, lo], axis=0)
    fine_table = np.concatenate([hi, hi, hi, lo, lo, low], axis=0)
    up = np.concatenate([2.0 * cosine[:, :HALF], -2.0 * sine[:, :HALF]], axis=1)
    up[:, 0] = 1.0
    up[:, HALF] = cosine[HALF]
    hi, lo = parts_of(up, 2)
    up_table = np.concatenate([hi, hi, lo], axis=1)
    ones = two_windows(np.ones((W, W))).astype(ml_dtypes.bfloat16)
    sum_table = np.concatenate([ones, ones, ones], axis=0)
    return down_table, across_table, fine_table, up_table, sum_table


def mxu(a, b):
    return jnp.dot(a, b, preferred_element_type=F32)


def split2(x):
    hi = x.astype(BF16)
    lo = (x - hi.astype(F32)).astype(BF16)
    return hi, lo


def split3(x):
    hi = x.astype(BF16)
    rest = x - hi.astype(F32)
    mid = rest.astype(BF16)
    low = (rest - mid.astype(F32)).astype(BF16)
    return hi, mid, low


def left32(x):
    return pltpu.roll(x, x.shape[1] - STRIDE, 1)


def eight_tiles(x, shifted):
    count = x.shape[1] // LANES - 1
    return [x[:, LANES * t : LANES * (t + 1)] for t in range(count)] + [
        shifted[:, LANES * t : LANES * (t + 1)] for t in range(count)
    ]


def window_rows(tile_ref, row_ref, col_ref, i, down_count):
    top = STRIDE * i
    lanes = tile_ref.shape[1]
    if i < down_count - 1:
        left = tile_ref[top : top + W, :]
    else:
        left = jnp.concatenate([tile_ref[top : top + STRIDE, :], row_ref[...]], axis=0)
    return jnp.concatenate([left, col_ref[top : top + W, :]], axis=1)


def forward(tile_ref, row_ref, col_ref, down_ref, across_ref, x_ref, stat_ref):
    down_count = x_ref.shape[0]
    tiles = x_ref.shape[1]
    for i in range(down_count):
        pixels = window_rows(tile_ref, row_ref, col_ref, i, down_count)
        base = pixels[0:1, :]
        above = pixels - base
        total = jnp.sum(above, axis=0, keepdims=True)
        centred = above - total * (1.0 / W)
        stat_ref[0, i : i + 1, :] = base
        stat_ref[1, i : i + 1, :] = total
        stat_ref[2, i : i + 1, :] = jnp.sum(centred * centred, axis=0, keepdims=True)
        hi, lo = split2(centred)
        columns = mxu(down_ref[...], jnp.concatenate([hi, lo, hi], axis=0))
        rows = []
        for tile in eight_tiles(columns, left32(columns)):
            hi, lo = split2(tile)
            rows.append(jnp.concatenate([hi, lo, hi], axis=1))
        spectrum = mxu(jnp.concatenate(rows, axis=0), across_ref[...])
        for k in range(tiles):
            block = spectrum[W * k : W * (k + 1)]
            x_ref[i, k, 0:HALF, :] = block[:HALF, :LANES] + block[HALF:, LANES:]
            x_ref[i, k, HALF:W, :] = block[HALF:, :LANES] - block[:HALF, LANES:]


def stacked(x):
    return jnp.concatenate(eight_tiles(x, left32(x)), axis=0)


def statistics(stat_ref, sum_ref, fine_ref):
    base = stacked(stat_ref[0])
    total = stacked(stat_ref[1])
    squares = stacked(stat_ref[2])
    mean_base = mxu(jnp.concatenate(split3(base), axis=1), sum_ref[...]) * (1.0 / W)
    level = total + float(W) * (base - mean_base)
    energy = squares + level * level * (1.0 / W)
    both = jnp.concatenate([level, energy], axis=0)
    sums = mxu(jnp.concatenate(split3(both), axis=1), sum_ref[...])
    count = level.shape[0]
    mean_level = sums[:count] * (1.0 / W)
    variance = (sums[count:] - mean_level * mean_level) * (1.0 / (W * W))
    scale = lax.rsqrt(jnp.maximum(variance, 0.0) + EPS)
    hi, mid, low = split3(level - mean_level)
    wave = mxu(jnp.concatenate([hi, mid, low, hi, mid, hi], axis=1), fine_ref[...])
    lane = lax.broadcasted_iota(jnp.int32, (count, LANES), 1)
    inside = lax.rem(lane, W) != 0
    real = jnp.where(inside, wave[:, :LANES], 0.0)
    imaginary = jnp.where(inside, -wave[:, LANES:], 0.0)
    return real, imaginary, scale


def frequency32(x_ref):
    down_count, tiles = x_ref.shape[0], x_ref.shape[1]
    minus = jnp.concatenate([x_ref[i, k, 0:1, :] for k in range(tiles) for i in range(down_count)], axis=0)
    real = jnp.concatenate([x_ref[i, k, HALF : HALF + 1, :] for k in range(tiles) for i in range(down_count)], axis=0)
    return real, -minus


def cross(a_real, a_imaginary, b_real, b_imaginary):
    return (
        a_real * b_real + a_imaginary * b_imaginary,
        a_real * b_imaginary - a_imaginary * b_real,
    )


def across_back(blocks, across_ref):
    rows = []
    for block in blocks:
        hi, lo = split2(block)
        rows.append(jnp.concatenate([hi, lo, hi], axis=1))
    return mxu(jnp.concatenate(rows, axis=0), across_ref[...])


def edge_rows(first_ref, second_ref, first_stat, second_stat, tables, edge_ref, scale_ref):
    down_ref, across_ref, fine_ref, up_ref, sum_ref = tables
    a_real, a_imaginary, a_scale = statistics(first_stat, sum_ref, fine_ref)
    b_real, b_imaginary, b_scale = statistics(second_stat, sum_ref, fine_ref)
    scale = a_scale * b_scale * (1.0 / (W * W * W))
    scale_ref[...] = scale
    p_real, p_imaginary = cross(a_real, a_imaginary, b_real, b_imaginary)
    r_real, r_imaginary = cross(*frequency32(first_ref), *frequency32(second_ref))
    back = across_back([p_real, p_imaginary, r_real, r_imaginary], across_ref)
    n = scale.shape[0]
    edge_ref[0] = (back[:n, :LANES] - back[n : 2 * n, LANES:]) * scale
    edge_ref[1] = (back[2 * n : 3 * n, :LANES] - back[3 * n :, LANES:]) * scale


def backward(first_ref, second_ref, across_ref, up_ref, edge_ref, scale_ref, out_ref):
    down_count, tiles = first_ref.shape[0], first_ref.shape[1]
    lane = lax.broadcasted_iota(jnp.int32, (W, LANES), 1)
    sublane = lax.broadcasted_iota(jnp.int32, (HALF, LANES), 0)
    left = lane < W
    for i in range(down_count):
        blocks = []
        for k in range(tiles):
            blocks.append(
                jnp.concatenate(
                    cross(
                        first_ref[i, k, 0:HALF, :],
                        first_ref[i, k, HALF:W, :],
                        second_ref[i, k, 0:HALF, :],
                        second_ref[i, k, HALF:W, :],
                    ),
                    axis=0,
                )
            )
        back = across_back(blocks, across_ref)
        lines = []
        for k in range(tiles):
            block = back[W * k : W * (k + 1)]
            at = down_count * k + i
            scale = scale_ref[at : at + 1, :]
            real = (block[:HALF, :LANES] - block[HALF:, LANES:]) * scale
            imaginary = (block[HALF:, :LANES] + block[:HALF, LANES:]) * scale
            real = jnp.where(sublane == 0, edge_ref[0, at : at + 1, :], real)
            imaginary = jnp.where(sublane == 0, edge_ref[1, at : at + 1, :], imaginary)
            lines.append(jnp.concatenate([real, imaginary], axis=0))
        pairs = []
        for t in range(tiles // 2):
            even, odd = lines[t], lines[tiles // 2 + t]
            pairs.append(jnp.where(left, even, pltpu.roll(odd, W, 1)))
            pairs.append(jnp.where(left, pltpu.roll(even, W, 1), odd))
        hi, lo = split2(jnp.concatenate(pairs, axis=1))
        out_ref[0, i] = mxu(up_ref[...], jnp.concatenate([hi, lo, hi], axis=0))


def whole_kernel(
    tile_ref, row_ref, col_ref, next_ref, next_row_ref, next_col_ref,
    down_ref, across_ref, fine_ref, up_ref, sum_ref,
    out_ref,
    first_ref, second_ref, first_stat, second_stat, edge_ref, scale_ref,
):
    tables = (down_ref, across_ref, fine_ref, up_ref, sum_ref)
    forward(tile_ref, row_ref, col_ref, down_ref, across_ref, first_ref, first_stat)
    forward(next_ref, next_row_ref, next_col_ref, down_ref, across_ref, second_ref, second_stat)
    edge_rows(first_ref, second_ref, first_stat, second_stat, tables, edge_ref, scale_ref)
    backward(first_ref, second_ref, across_ref, up_ref, edge_ref, scale_ref, out_ref)


def correlate(tile, row, col, following, next_row, next_col):
    height, breadth = tile.shape
    down_count = height // STRIDE
    tiles = 2 * breadth // LANES
    wide = breadth + LANES
    tables = [jnp.asarray(t, BF16) for t in make_tables()]
    scratch = [
        pltpu.VMEM((down_count, tiles, W, LANES), F32),
        pltpu.VMEM((down_count, tiles, W, LANES), F32),
        pltpu.VMEM((3, down_count, wide), F32),
        pltpu.VMEM((3, down_count, wide), F32),
        pltpu.VMEM((2, tiles * down_count, LANES), F32),
        pltpu.VMEM((tiles * down_count, LANES), F32),
    ]
    return pl.pallas_call(
        whole_kernel,
        out_shape=jax.ShapeDtypeStruct((1, down_count, W, 2 * breadth), F32),
        in_specs=[pl.BlockSpec(memory_space=pltpu.VMEM)] * 11,
        out_specs=pl.BlockSpec(memory_space=pltpu.VMEM),
        scratch_shapes=scratch,
        compiler_params=pltpu.CompilerParams(vmem_limit_bytes=40 << 20),
        name="correlate",
    )(tile, row, col, following, next_row, next_col, *tables)


def shifted(x, axis, by):
    devices = lax.axis_size(axis)
    pairs = [(i, i + by) for i in range(devices) if 0 <= i + by < devices]
    return lax.ppermute(x, axis, pairs)


def on_device(frames, following):
    at_end = lax.axis_index("tm") == lax.axis_size("tm") - 1
    tile = frames[0]
    arriving = shifted(tile, "tm", -1)
    both = jnp.stack([tile[:STRIDE], following[:STRIDE]])
    below = shifted(both, "row", -1)
    slab = jnp.concatenate([jnp.stack([tile, following])[:, :, :LANES], below[:, :, :LANES]], axis=1)
    beside = shifted(slab, "col", -1)
    next_row = jnp.where(at_end, below[1], shifted(below[0], "tm", -1))
    next_col = jnp.where(at_end, beside[1], shifted(beside[0], "tm", -1))
    upcoming = jnp.where(at_end, following, arriving)
    return correlate(tile, below[0], beside[0], upcoming, next_row, next_col)


def solution(mesh):
    in_specs = (P("tm", "row", "col"), P("row", "col"))
    out_specs = P("tm", "row", None, "col")
    return jax.shard_map(
        on_device, mesh=mesh, in_specs=in_specs, out_specs=out_specs, check_vma=False
    )
```

```python
import functools

import jax
import jax.numpy as jnp
import ml_dtypes
import numpy as np
from jax import lax
from jax.experimental import pallas as pl
from jax.experimental.pallas import tpu as pltpu
from jax.sharding import PartitionSpec as P


W = 64
STRIDE = 32
HALF = W // 2
LANES = 128
EPS = 1e-05
F32 = jnp.float32
BF16 = jnp.bfloat16
FIRST_VMEM = 8 << 20
SECOND_VMEM = 16 << 20


def parts_of(table, count):
    rest = np.asarray(table, np.float64)
    out = []
    for _ in range(count):
        part = rest.astype(ml_dtypes.bfloat16)
        out.append(part)
        rest = rest - part.astype(np.float64)
    return out


def two_windows(block):
    zero = np.zeros_like(block)
    return np.block([[block, zero], [zero, block]])


def make_tables():
    index = np.arange(W)
    turns = 2.0 * np.pi / W * (index[:, None] * index[None, :] % W)
    cosine, sine = np.cos(turns), np.sin(turns)
    down = np.concatenate([cosine[:HALF], -sine[:HALF]], axis=0)
    down[0] = 0.0
    down[HALF] = cosine[HALF]
    hi, lo = parts_of(down, 2)
    down_table = np.concatenate([hi, hi, lo], axis=1)
    across = np.concatenate([two_windows(cosine), two_windows(sine)], axis=1)
    hi, lo, low = parts_of(across, 3)
    across_table = np.concatenate([hi, hi, lo], axis=0)
    fine_table = np.concatenate([hi, hi, hi, lo, lo, low], axis=0)
    up = np.concatenate([2.0 * cosine[:, :HALF], -2.0 * sine[:, :HALF]], axis=1)
    up[:, 0] = 1.0
    up[:, HALF] = cosine[HALF]
    hi, lo = parts_of(up, 2)
    up_table = np.concatenate([hi, hi, lo], axis=1)
    ones = two_windows(np.ones((W, W))).astype(ml_dtypes.bfloat16)
    sum_table = np.concatenate([ones, ones, ones], axis=0)
    return down_table, across_table, fine_table, up_table, sum_table


def mxu(a, b):
    return jnp.dot(a, b, preferred_element_type=F32)


def split2(x):
    hi = x.astype(BF16)
    lo = (x - hi.astype(F32)).astype(BF16)
    return hi, lo


def split3(x):
    hi = x.astype(BF16)
    rest = x - hi.astype(F32)
    mid = rest.astype(BF16)
    low = (rest - mid.astype(F32)).astype(BF16)
    return hi, mid, low


def left32(x):
    return pltpu.roll(x, x.shape[1] - STRIDE, 1)


def eight_tiles(x, shifted):
    count = x.shape[1] // LANES - 1
    return [x[:, LANES * t : LANES * (t + 1)] for t in range(count)] + [
        shifted[:, LANES * t : LANES * (t + 1)] for t in range(count)
    ]


def column_block(pack, corner, b):
    blocks = 2 * LANES // STRIDE
    if b < blocks:
        return turned(pack[STRIDE * (b % 2) : STRIDE * (b % 2) + STRIDE, :], b // 2)
    return jnp.concatenate([turned(corner, q) for q in range(LANES // STRIDE)], axis=0)


def turned(x, quarter):
    return pltpu.roll(x, LANES - STRIDE * quarter, 1) if quarter else x


def window_rows(tile, rims, i, down_count):
    row, pack, corner = rims
    top = STRIDE * i
    if i < down_count - 1:
        left = tile[top : top + W, :]
    else:
        left = jnp.concatenate([tile[top : top + STRIDE, :], row], axis=0)
    right = jnp.concatenate([column_block(pack, corner, i), column_block(pack, corner, i + 1)], axis=0)
    return jnp.concatenate([left, right], axis=1)


def forward(tile, rims, down_ref, across_ref, x_ref, stat_ref):
    down_count = x_ref.shape[0]
    tiles = x_ref.shape[1]
    for i in range(down_count):
        pixels = window_rows(tile, rims, i, down_count)
        base = pixels[0:1, :]
        above = pixels - base
        total = jnp.sum(above, axis=0, keepdims=True)
        centred = above - total * (1.0 / W)
        stat_ref[0, i : i + 1, :] = base
        stat_ref[1, i : i + 1, :] = total
        stat_ref[2, i : i + 1, :] = jnp.sum(centred * centred, axis=0, keepdims=True)
        hi, lo = split2(centred)
        columns = mxu(down_ref[...], jnp.concatenate([hi, lo, hi], axis=0))
        rows = []
        for piece in eight_tiles(columns, left32(columns)):
            hi, lo = split2(piece)
            rows.append(jnp.concatenate([hi, lo, hi], axis=1))
        spectrum = mxu(jnp.concatenate(rows, axis=0), across_ref[...])
        for k in range(tiles):
            block = spectrum[W * k : W * (k + 1)]
            x_ref[i, k, 0:HALF, :] = block[:HALF, :LANES] + block[HALF:, LANES:]
            x_ref[i, k, HALF:W, :] = block[HALF:, :LANES] - block[:HALF, LANES:]


def stacked(x):
    return jnp.concatenate(eight_tiles(x, left32(x)), axis=0)


def statistics(stat_ref, sum_ref, fine_ref):
    base = stacked(stat_ref[0])
    total = stacked(stat_ref[1])
    squares = stacked(stat_ref[2])
    mean_base = mxu(jnp.concatenate(split3(base), axis=1), sum_ref[...]) * (1.0 / W)
    level = total + float(W) * (base - mean_base)
    energy = squares + level * level * (1.0 / W)
    both = jnp.concatenate([level, energy], axis=0)
    sums = mxu(jnp.concatenate(split3(both), axis=1), sum_ref[...])
    count = level.shape[0]
    mean_level = sums[:count] * (1.0 / W)
    variance = (sums[count:] - mean_level * mean_level) * (1.0 / (W * W))
    scale = lax.rsqrt(jnp.maximum(variance, 0.0) + EPS)
    hi, mid, low = split3(level - mean_level)
    wave = mxu(jnp.concatenate([hi, mid, low, hi, mid, hi], axis=1), fine_ref[...])
    lane = lax.broadcasted_iota(jnp.int32, (count, LANES), 1)
    inside = lax.rem(lane, W) != 0
    real = jnp.where(inside, wave[:, :LANES], 0.0)
    imaginary = jnp.where(inside, -wave[:, LANES:], 0.0)
    return real, imaginary, scale


def frequency32(x_ref):
    down_count, tiles = x_ref.shape[0], x_ref.shape[1]
    minus = jnp.concatenate([x_ref[i, k, 0:1, :] for k in range(tiles) for i in range(down_count)], axis=0)
    real = jnp.concatenate([x_ref[i, k, HALF : HALF + 1, :] for k in range(tiles) for i in range(down_count)], axis=0)
    return real, -minus


def cross(a_real, a_imaginary, b_real, b_imaginary):
    return (
        a_real * b_real + a_imaginary * b_imaginary,
        a_real * b_imaginary - a_imaginary * b_real,
    )


def across_back(blocks, across_ref):
    rows = []
    for block in blocks:
        hi, lo = split2(block)
        rows.append(jnp.concatenate([hi, lo, hi], axis=1))
    return mxu(jnp.concatenate(rows, axis=0), across_ref[...])


def edge_rows(first_ref, second_ref, first_stat, second_stat, tables, edge_ref, scale_ref):
    _, across_ref, fine_ref, _, sum_ref = tables
    a_real, a_imaginary, a_scale = statistics(first_stat, sum_ref, fine_ref)
    b_real, b_imaginary, b_scale = statistics(second_stat, sum_ref, fine_ref)
    scale = a_scale * b_scale * (1.0 / (W * W * W))
    scale_ref[...] = scale
    p_real, p_imaginary = cross(a_real, a_imaginary, b_real, b_imaginary)
    r_real, r_imaginary = cross(*frequency32(first_ref), *frequency32(second_ref))
    back = across_back([p_real, p_imaginary, r_real, r_imaginary], across_ref)
    n = scale.shape[0]
    edge_ref[0] = (back[:n, :LANES] - back[n : 2 * n, LANES:]) * scale
    edge_ref[1] = (back[2 * n : 3 * n, :LANES] - back[3 * n :, LANES:]) * scale


def backward(first_ref, second_ref, across_ref, up_ref, edge_ref, scale_ref, out_ref, finished):
    down_count, tiles = first_ref.shape[0], first_ref.shape[1]
    lane = lax.broadcasted_iota(jnp.int32, (W, LANES), 1)
    sublane = lax.broadcasted_iota(jnp.int32, (HALF, LANES), 0)
    left = lane < W
    for i in range(down_count):
        blocks = []
        for k in range(tiles):
            blocks.append(
                jnp.concatenate(
                    cross(
                        first_ref[i, k, 0:HALF, :],
                        first_ref[i, k, HALF:W, :],
                        second_ref[i, k, 0:HALF, :],
                        second_ref[i, k, HALF:W, :],
                    ),
                    axis=0,
                )
            )
        back = across_back(blocks, across_ref)
        lines = []
        for k in range(tiles):
            block = back[W * k : W * (k + 1)]
            at = down_count * k + i
            scale = scale_ref[at : at + 1, :]
            real = (block[:HALF, :LANES] - block[HALF:, LANES:]) * scale
            imaginary = (block[HALF:, :LANES] + block[:HALF, LANES:]) * scale
            real = jnp.where(sublane == 0, edge_ref[0, at : at + 1, :], real)
            imaginary = jnp.where(sublane == 0, edge_ref[1, at : at + 1, :], imaginary)
            lines.append(jnp.concatenate([real, imaginary], axis=0))
        pairs = []
        for t in range(tiles // 2):
            even, odd = lines[t], lines[tiles // 2 + t]
            pairs.append(jnp.where(left, even, pltpu.roll(odd, W, 1)))
            pairs.append(jnp.where(left, pltpu.roll(even, W, 1), odd))
        hi, lo = split2(jnp.concatenate(pairs, axis=1))
        out_ref[i] = mxu(up_ref[...], jnp.concatenate([hi, lo, hi], axis=0))
        finished(i)


def packed_columns(x):
    rows = x.shape[0] // 4
    lane = lax.broadcasted_iota(jnp.int32, (rows, LANES), 1)
    out = x[:rows]
    for q in range(1, 4):
        out = jnp.where(lane < STRIDE * q, out, pltpu.roll(x[rows * q : rows * (q + 1)], STRIDE * q, 1))
    return out


def strips_kernel(row_ref, col_ref, next_row_ref, next_col_ref, out_row_ref, out_col_ref, out_corner_ref):
    for n, (row, col) in enumerate(((row_ref, col_ref), (next_row_ref, next_col_ref))):
        out_row_ref[n] = row[...].reshape(row.shape[-2:])
        slab = col[...].reshape(col.shape[-2:])
        out_col_ref[n] = packed_columns(slab)
        out_corner_ref[n] = packed_columns(slab[:STRIDE])


def strips(frames, following):
    height, breadth = following.shape
    return pl.pallas_call(
        strips_kernel,
        grid=(1,),
        out_shape=(
            jax.ShapeDtypeStruct((2, STRIDE, breadth), F32),
            jax.ShapeDtypeStruct((2, height // 4, LANES), F32),
            jax.ShapeDtypeStruct((2, STRIDE // 4, LANES), F32),
        ),
        in_specs=[
            pl.BlockSpec((1, STRIDE, breadth), lambda g: (0, 0, 0)),
            pl.BlockSpec((1, height, LANES), lambda g: (0, 0, 0)),
            pl.BlockSpec((STRIDE, breadth), lambda g: (0, 0)),
            pl.BlockSpec((height, LANES), lambda g: (0, 0)),
        ],
        out_specs=(
            pl.BlockSpec((2, STRIDE, breadth), lambda g: (0, 0, 0)),
            pl.BlockSpec((2, height // 4, LANES), lambda g: (0, 0, 0)),
            pl.BlockSpec((2, STRIDE // 4, LANES), lambda g: (0, 0, 0)),
        ),
        name="strips",
    )(frames, frames, following, following)


def first_kernel(lasts, tile_ref, row_ref, col_ref, corner_ref, down_ref, across_ref, x_ref, stat_ref, send_ref, next_ref):
    row_last, col_last = lasts()
    for n, out in enumerate((send_ref, next_ref)):
        row = jnp.where(row_last, 0.0, row_ref[n])
        pack = jnp.where(col_last, 0.0, col_ref[n])
        corner = jnp.where(jnp.logical_or(row_last, col_last), 0.0, corner_ref[n])
        pieces = [row[:, LANES * t : LANES * (t + 1)] for t in range(row.shape[1] // LANES)]
        out[...] = jnp.concatenate(pieces + [pack, corner], axis=0)
        if n == 0:
            rims = (row, pack, corner)
    forward(tile_ref[...], rims, down_ref, across_ref, x_ref, stat_ref)


def second_kernel(
    at_end, tile_ref, following_ref, rim_ref, following_rim_ref, first_ref, first_stat,
    down_ref, across_ref, fine_ref, up_ref, sum_ref,
    out_ref,
    second_ref, second_stat, edge_ref, scale_ref, plane_ref, sems,
):
    last = at_end()
    tile = jnp.where(last, following_ref[...], tile_ref[...])
    rim = jnp.where(last, following_rim_ref[...], rim_ref[...])
    tables = (down_ref, across_ref, fine_ref, up_ref, sum_ref)
    count = tile.shape[1] // LANES
    row = jnp.concatenate([rim[STRIDE * t : STRIDE * (t + 1)] for t in range(count)], axis=1)
    at = STRIDE * count
    rows = tile.shape[0] // 4
    rims = (row, rim[at : at + rows], rim[at + rows : at + rows + STRIDE // 4])
    forward(tile, rims, down_ref, across_ref, second_ref, second_stat)
    edge_rows(first_ref, second_ref, first_stat, second_stat, tables, edge_ref, scale_ref)
    copies = []

    def finished(i):
        copies.append(pltpu.make_async_copy(plane_ref.at[i], out_ref.at[0, i], sems.at[i]))
        copies[-1].start()

    backward(first_ref, second_ref, across_ref, up_ref, edge_ref, scale_ref, plane_ref, finished)
    for copy in copies:
        copy.wait()


ANY = pl.BlockSpec(memory_space=pl.ANY)
VMEM = pl.BlockSpec(memory_space=pltpu.VMEM)


def sizes(height, breadth):
    down_count = height // STRIDE
    tiles = 2 * breadth // LANES
    spectrum = (down_count, tiles, W, LANES)
    stat = (3, down_count, breadth + LANES)
    rim = (STRIDE * (breadth // LANES) + height // 4 + STRIDE // 4, LANES)
    return down_count, tiles, spectrum, stat, rim


def first(tile, row, col, corner, lasts, tables):
    _, _, spectrum, stat, rim = sizes(*tile.shape)
    return pl.pallas_call(
        functools.partial(first_kernel, lasts),
        out_shape=tuple(jax.ShapeDtypeStruct(shape, F32) for shape in (spectrum, stat, rim, rim)),
        in_specs=[VMEM] * 6,
        out_specs=(VMEM,) * 4,
        compiler_params=pltpu.CompilerParams(vmem_limit_bytes=FIRST_VMEM),
        cost_estimate=pl.CostEstimate(flops=3 * 10**9, bytes_accessed=3 << 20, transcendentals=0),
        name="first",
    )(tile, row, col, corner, *tables[:2])


def second(at_end, tile, following, rims, following_rims, spectrum, stat, tables):
    height, breadth = tile.shape
    down_count, tiles, shape, stat_shape, _ = sizes(height, breadth)
    return pl.pallas_call(
        functools.partial(second_kernel, at_end),
        out_shape=jax.ShapeDtypeStruct((1, down_count, W, 2 * breadth), F32),
        in_specs=[VMEM] * 11,
        out_specs=ANY,
        scratch_shapes=[
            pltpu.VMEM(shape, F32),
            pltpu.VMEM(stat_shape, F32),
            pltpu.VMEM((2, tiles * down_count, LANES), F32),
            pltpu.VMEM((tiles * down_count, LANES), F32),
            pltpu.VMEM((down_count, W, 2 * breadth), F32),
            pltpu.SemaphoreType.DMA((down_count,)),
        ],
        compiler_params=pltpu.CompilerParams(vmem_limit_bytes=SECOND_VMEM),
        cost_estimate=pl.CostEstimate(flops=8 * 10**9, bytes_accessed=5 << 20, transcendentals=0),
        name="second",
    )(tile, following, rims, following_rims, spectrum, stat, *tables)


def shifted(x, axis, by):
    devices = lax.axis_size(axis)
    pairs = [(i, i + by) for i in range(devices) if 0 <= i + by < devices]
    return lax.ppermute(x, axis, pairs)


def turned_down(x, *axes):
    counts = [lax.axis_size(axis) for axis in axes]
    pairs = []
    for source in np.ndindex(*counts):
        target = tuple((s - 1) % n for s, n in zip(source, counts))
        pairs.append((int(np.ravel_multi_index(source, counts)), int(np.ravel_multi_index(target, counts))))
    return lax.ppermute(x, axes if len(axes) > 1 else axes[0], pairs)


def lasts():
    return (
        lax.axis_index("row") == lax.axis_size("row") - 1,
        lax.axis_index("col") == lax.axis_size("col") - 1,
    )


def at_end():
    return lax.axis_index("tm") == lax.axis_size("tm") - 1


def on_device(frames, following):
    tables = [jnp.asarray(t, BF16) for t in make_tables()]
    tile = frames[0]
    arriving = shifted(tile, "tm", -1)
    rows, cols, corners = strips(frames, following)
    rows = turned_down(rows, "row")
    cols = turned_down(cols, "col")
    corners = turned_down(corners, "row", "col")
    spectrum, stat, send, following_rims = first(tile, rows, cols, corners, lasts, tables)
    rims = shifted(send, "tm", -1)
    return second(at_end, arriving, following, rims, following_rims, spectrum, stat, tables)


def solution(mesh):
    in_specs = (P("tm", "row", "col"), P("row", "col"))
    out_specs = P("tm", "row", None, "col")


    return jax.shard_map(
        on_device, mesh=mesh, in_specs=in_specs, out_specs=out_specs, check_vma=False
    )
```

```python
import functools

import jax
import jax.numpy as jnp
import ml_dtypes
import numpy as np
from jax import lax
from jax.experimental import pallas as pl
from jax.experimental.pallas import tpu as pltpu
from jax.sharding import PartitionSpec as P


W = 64
STRIDE = 32
HALF = W // 2
LANES = 128
EPS = 1e-05
F32 = jnp.float32
BF16 = jnp.bfloat16
ANY = pl.BlockSpec(memory_space=pl.ANY)
VMEM = pl.BlockSpec(memory_space=pltpu.VMEM)
STRIPS_VMEM = 60 << 20
FIRST_VMEM = 8 << 20
SECOND_VMEM = 16 << 20


def parts_of(table, count):
    rest = np.asarray(table, np.float64)
    out = []
    for _ in range(count):
        part = rest.astype(ml_dtypes.bfloat16)
        out.append(part)
        rest = rest - part.astype(np.float64)
    return out


def two_windows(block):
    zero = np.zeros_like(block)
    return np.block([[block, zero], [zero, block]])


def make_tables():
    index = np.arange(W)
    turns = 2.0 * np.pi / W * (index[:, None] * index[None, :] % W)
    cosine, sine = np.cos(turns), np.sin(turns)
    down = np.concatenate([cosine[:HALF], -sine[:HALF]], axis=0)
    down[0] = 0.0
    down[HALF] = cosine[HALF]
    hi, lo = parts_of(down, 2)
    down_table = np.concatenate([hi, hi, lo], axis=1)
    across = np.concatenate([two_windows(cosine), two_windows(sine)], axis=1)
    hi, lo, low = parts_of(across, 3)
    across_table = np.concatenate([hi, hi, lo], axis=0)
    fine_table = np.concatenate([hi, hi, hi, lo, lo, low], axis=0)
    up = np.concatenate([2.0 * cosine[:, :HALF], -2.0 * sine[:, :HALF]], axis=1)
    up[:, 0] = 1.0
    up[:, HALF] = cosine[HALF]
    hi, lo = parts_of(up, 2)
    up_table = np.concatenate([hi, hi, lo], axis=1)
    ones = two_windows(np.ones((W, W))).astype(ml_dtypes.bfloat16)
    sum_table = np.concatenate([ones, ones, ones], axis=0)
    return down_table, across_table, fine_table, up_table, sum_table


def mxu(a, b):
    return jnp.dot(a, b, preferred_element_type=F32)


def split2(x):
    hi = x.astype(BF16)
    lo = (x - hi.astype(F32)).astype(BF16)
    return hi, lo


def split3(x):
    hi = x.astype(BF16)
    rest = x - hi.astype(F32)
    mid = rest.astype(BF16)
    low = (rest - mid.astype(F32)).astype(BF16)
    return hi, mid, low


def left32(x):
    return pltpu.roll(x, x.shape[1] - STRIDE, 1)


def eight_tiles(x, shifted):
    count = x.shape[1] // LANES - 1
    return [x[:, LANES * t : LANES * (t + 1)] for t in range(count)] + [
        shifted[:, LANES * t : LANES * (t + 1)] for t in range(count)
    ]


def column_block(pack, corner, b):
    blocks = 2 * LANES // STRIDE
    if b == blocks:
        return corner
    block = pack[STRIDE * (b % 2) : STRIDE * (b % 2) + STRIDE]
    return pltpu.roll(block, LANES - STRIDE * (b // 2), 1) if b // 2 else block


def window_rows(tile, rims, i, down_count):
    row, pack, corner = rims
    top = STRIDE * i
    if i < down_count - 1:
        left = tile[top : top + W, :]
    else:
        left = jnp.concatenate([tile[top : top + STRIDE, :], row], axis=0)
    right = jnp.concatenate([column_block(pack, corner, i), column_block(pack, corner, i + 1)], axis=0)
    return jnp.concatenate([left, right], axis=1)


def forward(tile, rims, down_ref, across_ref, x_ref, stat_ref):
    down_count = x_ref.shape[0]
    tiles = x_ref.shape[1]
    for i in range(down_count):
        pixels = window_rows(tile, rims, i, down_count)
        base = pixels[0:1, :]
        above = pixels - base
        total = jnp.sum(above, axis=0, keepdims=True)
        centred = above - total * (1.0 / W)
        stat_ref[0, i : i + 1, :] = base
        stat_ref[1, i : i + 1, :] = total
        stat_ref[2, i : i + 1, :] = jnp.sum(centred * centred, axis=0, keepdims=True)
        hi, lo = split2(centred)
        columns = mxu(down_ref[...], jnp.concatenate([hi, lo, hi], axis=0))
        rows = []
        for piece in eight_tiles(columns, left32(columns)):
            hi, lo = split2(piece)
            rows.append(jnp.concatenate([hi, lo, hi], axis=1))
        spectrum = mxu(jnp.concatenate(rows, axis=0), across_ref[...])
        for k in range(tiles):
            block = spectrum[W * k : W * (k + 1)]
            x_ref[i, k, 0:HALF, :] = block[:HALF, :LANES] + block[HALF:, LANES:]
            x_ref[i, k, HALF:W, :] = block[HALF:, :LANES] - block[:HALF, LANES:]


def stacked(x):
    return jnp.concatenate(eight_tiles(x, left32(x)), axis=0)


def statistics(stat_ref, sum_ref, fine_ref):
    base = stacked(stat_ref[0])
    total = stacked(stat_ref[1])
    squares = stacked(stat_ref[2])
    mean_base = mxu(jnp.concatenate(split3(base), axis=1), sum_ref[...]) * (1.0 / W)
    level = total + float(W) * (base - mean_base)
    energy = squares + level * level * (1.0 / W)
    both = jnp.concatenate([level, energy], axis=0)
    sums = mxu(jnp.concatenate(split3(both), axis=1), sum_ref[...])
    count = level.shape[0]
    mean_level = sums[:count] * (1.0 / W)
    variance = (sums[count:] - mean_level * mean_level) * (1.0 / (W * W))
    scale = lax.rsqrt(jnp.maximum(variance, 0.0) + EPS)
    hi, mid, low = split3(level - mean_level)
    wave = mxu(jnp.concatenate([hi, mid, low, hi, mid, hi], axis=1), fine_ref[...])
    lane = lax.broadcasted_iota(jnp.int32, (count, LANES), 1)
    inside = lax.rem(lane, W) != 0
    real = jnp.where(inside, wave[:, :LANES], 0.0)
    imaginary = jnp.where(inside, -wave[:, LANES:], 0.0)
    return real, imaginary, scale


def frequency32(x_ref):
    down_count, tiles = x_ref.shape[0], x_ref.shape[1]
    minus = jnp.concatenate([x_ref[i, k, 0:1, :] for k in range(tiles) for i in range(down_count)], axis=0)
    real = jnp.concatenate([x_ref[i, k, HALF : HALF + 1, :] for k in range(tiles) for i in range(down_count)], axis=0)
    return real, -minus


def cross(a_real, a_imaginary, b_real, b_imaginary):
    return (
        a_real * b_real + a_imaginary * b_imaginary,
        a_real * b_imaginary - a_imaginary * b_real,
    )


def across_back(blocks, across_ref):
    rows = []
    for block in blocks:
        hi, lo = split2(block)
        rows.append(jnp.concatenate([hi, lo, hi], axis=1))
    return mxu(jnp.concatenate(rows, axis=0), across_ref[...])


def edge_rows(first_ref, second_ref, first_stat, second_stat, tables, edge_ref, scale_ref):
    _, across_ref, fine_ref, _, sum_ref = tables
    a_real, a_imaginary, a_scale = statistics(first_stat, sum_ref, fine_ref)
    b_real, b_imaginary, b_scale = statistics(second_stat, sum_ref, fine_ref)
    scale = a_scale * b_scale * (1.0 / (W * W * W))
    scale_ref[...] = scale
    p_real, p_imaginary = cross(a_real, a_imaginary, b_real, b_imaginary)
    r_real, r_imaginary = cross(*frequency32(first_ref), *frequency32(second_ref))
    back = across_back([p_real, p_imaginary, r_real, r_imaginary], across_ref)
    n = scale.shape[0]
    edge_ref[0] = (back[:n, :LANES] - back[n : 2 * n, LANES:]) * scale
    edge_ref[1] = (back[2 * n : 3 * n, :LANES] - back[3 * n :, LANES:]) * scale


def backward(first_ref, second_ref, across_ref, up_ref, edge_ref, scale_ref, out_ref, finished):
    down_count, tiles = first_ref.shape[0], first_ref.shape[1]
    lane = lax.broadcasted_iota(jnp.int32, (W, LANES), 1)
    sublane = lax.broadcasted_iota(jnp.int32, (HALF, LANES), 0)
    left = lane < W
    for i in range(down_count):
        blocks = []
        for k in range(tiles):
            blocks.append(
                jnp.concatenate(
                    cross(
                        first_ref[i, k, 0:HALF, :],
                        first_ref[i, k, HALF:W, :],
                        second_ref[i, k, 0:HALF, :],
                        second_ref[i, k, HALF:W, :],
                    ),
                    axis=0,
                )
            )
        back = across_back(blocks, across_ref)
        lines = []
        for k in range(tiles):
            block = back[W * k : W * (k + 1)]
            at = down_count * k + i
            scale = scale_ref[at : at + 1, :]
            real = (block[:HALF, :LANES] - block[HALF:, LANES:]) * scale
            imaginary = (block[HALF:, :LANES] + block[:HALF, LANES:]) * scale
            real = jnp.where(sublane == 0, edge_ref[0, at : at + 1, :], real)
            imaginary = jnp.where(sublane == 0, edge_ref[1, at : at + 1, :], imaginary)
            lines.append(jnp.concatenate([real, imaginary], axis=0))
        pairs = []
        for t in range(tiles // 2):
            even, odd = lines[t], lines[tiles // 2 + t]
            pairs.append(jnp.where(left, even, pltpu.roll(odd, W, 1)))
            pairs.append(jnp.where(left, pltpu.roll(even, W, 1), odd))
        hi, lo = split2(jnp.concatenate(pairs, axis=1))
        out_ref[i] = mxu(up_ref[...], jnp.concatenate([hi, lo, hi], axis=0))
        finished(i)


def packed_columns(x):
    rows = x.shape[0] // 4
    lane = lax.broadcasted_iota(jnp.int32, (rows, LANES), 1)
    out = x[:rows]
    for q in range(1, 4):
        out = jnp.where(lane < STRIDE * q, out, pltpu.roll(x[rows * q : rows * (q + 1)], STRIDE * q, 1))
    return out


def strips_kernel(row_ref, slab_ref, next_row_ref, next_slab_ref, out_row_ref, out_col_ref):
    for n, (row, slab) in enumerate(((row_ref, slab_ref), (next_row_ref, next_slab_ref))):
        out_col_ref[n] = packed_columns(slab[...])
        for t in range(row.shape[1] // LANES):
            out_row_ref[n, STRIDE * t : STRIDE * (t + 1), :] = row[:, LANES * t : LANES * (t + 1)]


def strips(tile, following):
    height, breadth = following.shape
    ends = [
        pl.BlockSpec((STRIDE, breadth), lambda g: (0, 0)),
        pl.BlockSpec((height, LANES), lambda g: (0, 0)),
    ]
    return pl.pallas_call(
        strips_kernel,
        grid=(1,),
        out_shape=(
            jax.ShapeDtypeStruct((2, STRIDE * (breadth // LANES), LANES), F32),
            jax.ShapeDtypeStruct((2, height // 4, LANES), F32),
        ),
        in_specs=ends * 2,
        out_specs=(VMEM, VMEM),
        compiler_params=pltpu.CompilerParams(vmem_limit_bytes=STRIPS_VMEM),
        name="strips",
    )(tile, tile, following, following)


def join_kernel(upper_ref, lower_ref, out_ref):
    height = upper_ref.shape[-2]
    rows = out_ref.shape[-2] - height
    if len(out_ref.shape) == 3:
        out_ref[:, :height, :] = upper_ref[...]
        out_ref[:, height:, :] = lower_ref[:, :rows, :]
    else:
        out_ref[:height, :] = upper_ref[0]
        out_ref[height:, :] = lower_ref[0, :rows, :]


def join(upper, lower, shape):
    return pl.pallas_call(
        join_kernel,
        out_shape=jax.ShapeDtypeStruct(shape, F32),
        in_specs=[VMEM, VMEM],
        out_specs=VMEM,
        compiler_params=pltpu.CompilerParams(vmem_limit_bytes=2 << 20),
    )(upper, lower)


def rims_of(rows, cols, row_last, col_last, tall):
    tiles = jnp.where(row_last, 0.0, rows[:tall])
    row = jnp.concatenate([tiles[STRIDE * t : STRIDE * (t + 1)] for t in range(tall // STRIDE)], axis=1)
    corner = jnp.where(jnp.logical_or(row_last, col_last), 0.0, rows[tall:])
    return row, jnp.where(col_last, 0.0, cols), corner


def first_kernel(place, tile_ref, row_ref, col_ref, down_ref, across_ref, x_ref, stat_ref):
    row_last, col_last, _ = place()
    tall = STRIDE * (tile_ref.shape[1] // LANES)
    rims = rims_of(row_ref[0], col_ref[0], row_last, col_last, tall)
    forward(tile_ref[...], rims, down_ref, across_ref, x_ref, stat_ref)


def second_kernel(
    place, tile_ref, following_ref, rim_ref, row_ref, col_ref, first_ref, first_stat,
    down_ref, across_ref, fine_ref, up_ref, sum_ref,
    out_ref,
    second_ref, second_stat, edge_ref, scale_ref, plane_ref, sems,
):
    row_last, col_last, last = place()
    tile = jnp.where(last, following_ref[...], tile_ref[...])
    at = row_ref.shape[1]
    rows = jnp.where(last, row_ref[1], rim_ref[0:at, :])
    cols = jnp.where(last, col_ref[1], rim_ref[at:, :])
    tables = (down_ref, across_ref, fine_ref, up_ref, sum_ref)
    rims = rims_of(rows, cols, row_last, col_last, at - STRIDE)
    forward(tile, rims, down_ref, across_ref, second_ref, second_stat)
    edge_rows(first_ref, second_ref, first_stat, second_stat, tables, edge_ref, scale_ref)
    copies = []

    def finished(i):
        copies.append(pltpu.make_async_copy(plane_ref.at[i], out_ref.at[0, i], sems.at[i]))
        copies[-1].start()

    backward(first_ref, second_ref, across_ref, up_ref, edge_ref, scale_ref, plane_ref, finished)
    for copy in copies:
        copy.wait()


def sizes(height, breadth):
    down_count = height // STRIDE
    tiles = 2 * breadth // LANES
    return down_count, tiles, (down_count, tiles, W, LANES), (3, down_count, breadth + LANES)


def first(place, tile, rows, cols, tables):
    _, _, spectrum, stat = sizes(*tile.shape)
    return pl.pallas_call(
        functools.partial(first_kernel, place),
        out_shape=tuple(jax.ShapeDtypeStruct(shape, F32) for shape in (spectrum, stat)),
        in_specs=[VMEM] * 5,
        out_specs=(VMEM,) * 2,
        compiler_params=pltpu.CompilerParams(vmem_limit_bytes=FIRST_VMEM),
        cost_estimate=pl.CostEstimate(flops=3 * 10**9, bytes_accessed=3 << 20, transcendentals=0),
        name="first",
    )(tile, rows, cols, *tables[:2])


def second(place, tile, following, rims, rows, cols, spectrum, stat, tables):
    height, breadth = tile.shape
    down_count, tiles, shape, stat_shape = sizes(height, breadth)
    return pl.pallas_call(
        functools.partial(second_kernel, place),
        out_shape=jax.ShapeDtypeStruct((1, down_count, W, 2 * breadth), F32),
        in_specs=[VMEM] * 12,
        out_specs=ANY,
        scratch_shapes=[
            pltpu.VMEM(shape, F32),
            pltpu.VMEM(stat_shape, F32),
            pltpu.VMEM((2, tiles * down_count, LANES), F32),
            pltpu.VMEM((tiles * down_count, LANES), F32),
            pltpu.VMEM((down_count, W, 2 * breadth), F32),
            pltpu.SemaphoreType.DMA((down_count,)),
        ],
        compiler_params=pltpu.CompilerParams(vmem_limit_bytes=SECOND_VMEM),
        cost_estimate=pl.CostEstimate(flops=8 * 10**9, bytes_accessed=5 << 20, transcendentals=0),
        name="second",
    )(tile, following, rims, rows, cols, spectrum, stat, *tables)


def turned_down(x, axis):
    devices = lax.axis_size(axis)
    return lax.ppermute(x, axis, [(i, (i - 1) % devices) for i in range(devices)])


def place():
    return tuple(lax.axis_index(axis) == lax.axis_size(axis) - 1 for axis in ("row", "col", "tm"))


def on_device(frames, following):
    tables = [jnp.asarray(t, BF16) for t in make_tables()]
    tile = frames[0]
    rows, cols = strips(tile, following)
    cols = turned_down(cols, "col")
    arriving = turned_down(tile, "tm")
    tall = rows.shape[1]
    rows = turned_down(join(rows, cols, (2, tall + STRIDE, LANES)), "row")
    whole = (tall + STRIDE + cols.shape[1], LANES)
    rims = turned_down(join(rows, cols, whole), "tm")
    spectrum, stat = first(place, tile, rows, cols, tables)
    return second(place, arriving, following, rims, rows, cols, spectrum, stat, tables)


def solution(mesh):
    in_specs = (P("tm", "row", "col"), P("row", "col"))
    out_specs = P("tm", "row", None, "col")


    return jax.shard_map(
        on_device, mesh=mesh, in_specs=in_specs, out_specs=out_specs, check_vma=False
    )
```

```python
import functools

import jax
import jax.numpy as jnp
import ml_dtypes
import numpy as np
from jax import lax
from jax.experimental import pallas as pl
from jax.experimental.pallas import tpu as pltpu
from jax.sharding import PartitionSpec as P


W = 64
STRIDE = 32
HALF = W // 2
LANES = 128
EPS = 1e-05
F32 = jnp.float32
BF16 = jnp.bfloat16
LAG = 3
GROUP = 1
ANY = pl.BlockSpec(memory_space=pl.ANY)
VMEM = pl.BlockSpec(memory_space=pltpu.VMEM)
STRIPS_VMEM = 4 << 20
SMALL_VMEM = 2 << 20
FIRST_VMEM = 8 << 20
SECOND_VMEM = 16 << 20


def parts_of(table, count):
    rest = np.asarray(table, np.float64)
    out = []
    for _ in range(count):
        part = rest.astype(ml_dtypes.bfloat16)
        out.append(part)
        rest = rest - part.astype(np.float64)
    return out


def two_windows(block):
    zero = np.zeros_like(block)
    return np.block([[block, zero], [zero, block]])


def make_tables():
    index = np.arange(W)
    turns = 2.0 * np.pi / W * (index[:, None] * index[None, :] % W)
    cosine, sine = np.cos(turns), np.sin(turns)
    down = np.concatenate([cosine[:HALF], -sine[:HALF]], axis=0)
    down[0] = 0.0
    down[HALF] = cosine[HALF]
    hi, lo = parts_of(down, 2)
    down_table = np.concatenate([hi, hi, lo], axis=1)
    across = np.concatenate([two_windows(cosine), two_windows(sine)], axis=1)
    hi, lo, low = parts_of(across, 3)
    across_table = np.concatenate([hi, hi, lo], axis=0)
    fine_table = np.concatenate([hi, hi, hi, lo, lo, low], axis=0)
    up = np.concatenate([2.0 * cosine[:, :HALF], -2.0 * sine[:, :HALF]], axis=1)
    up[:, 0] = 1.0
    up[:, HALF] = cosine[HALF]
    hi, lo = parts_of(up, 2)
    up_table = np.concatenate([hi, hi, lo], axis=1)
    ones = two_windows(np.ones((W, W))).astype(ml_dtypes.bfloat16)
    sum_table = np.concatenate([ones, ones, ones], axis=0)
    tables = (down_table, across_table, fine_table, up_table, sum_table)
    return np.concatenate([np.pad(t, ((0, 0), (0, TABLE_LANES - t.shape[1]))) for t in tables], axis=0)


TABLES = ((W, 3 * W), (3 * LANES, 2 * LANES), (6 * LANES, 2 * LANES), (W, 3 * W), (3 * LANES, LANES))
TABLE_LANES = 2 * LANES


def table_refs(ref):
    out, at = [], 0
    for rows, lanes in TABLES:
        out.append(ref.at[at : at + rows, 0:lanes])
        at += rows
    return out


def mxu(a, b):
    return jnp.dot(a, b, preferred_element_type=F32)


def split2(x):
    hi = x.astype(BF16)
    lo = (x - hi.astype(F32)).astype(BF16)
    return hi, lo


def split3(x):
    hi = x.astype(BF16)
    rest = x - hi.astype(F32)
    mid = rest.astype(BF16)
    low = (rest - mid.astype(F32)).astype(BF16)
    return hi, mid, low


def left32(x):
    return pltpu.roll(x, x.shape[1] - STRIDE, 1)


def eight_tiles(x, shifted):
    count = x.shape[1] // LANES - 1
    return [x[:, LANES * t : LANES * (t + 1)] for t in range(count)] + [
        shifted[:, LANES * t : LANES * (t + 1)] for t in range(count)
    ]


def column_block(pack, corner, b):
    blocks = 2 * LANES // STRIDE
    if b == blocks:
        return jnp.concatenate([quarter(corner, q) for q in range(LANES // STRIDE)], axis=0)
    return quarter(pack[STRIDE * (b % 2) : STRIDE * (b % 2) + STRIDE], b // 2)


def quarter(x, q):
    return pltpu.roll(x, LANES - STRIDE * q, 1) if q else x


def window_rows(tile, rims, i, down_count):
    row, pack, corner = rims
    top = STRIDE * i
    if i < down_count - 1:
        left = tile[top : top + W, :]
    else:
        left = jnp.concatenate([tile[top : top + STRIDE, :], row], axis=0)
    right = jnp.concatenate([column_block(pack, corner, i), column_block(pack, corner, i + 1)], axis=0)
    return jnp.concatenate([left, right], axis=1)


def forward(tile, rims, down_ref, across_ref, x_ref, stat_ref):
    down_count = x_ref.shape[0]
    tiles = x_ref.shape[1]
    for i in range(down_count):
        pixels = window_rows(tile, rims, i, down_count)
        base = pixels[0:1, :]
        above = pixels - base
        total = jnp.sum(above, axis=0, keepdims=True)
        centred = above - total * (1.0 / W)
        stat_ref[0, i : i + 1, :] = base
        stat_ref[1, i : i + 1, :] = total
        stat_ref[2, i : i + 1, :] = jnp.sum(centred * centred, axis=0, keepdims=True)
        hi, lo = split2(centred)
        columns = mxu(down_ref[...], jnp.concatenate([hi, lo, hi], axis=0))
        rows = []
        for piece in eight_tiles(columns, left32(columns)):
            hi, lo = split2(piece)
            rows.append(jnp.concatenate([hi, lo, hi], axis=1))
        spectrum = mxu(jnp.concatenate(rows, axis=0), across_ref[...])
        for k in range(tiles):
            block = spectrum[W * k : W * (k + 1)]
            x_ref[i, k, 0:HALF, :] = block[:HALF, :LANES] + block[HALF:, LANES:]
            x_ref[i, k, HALF:W, :] = block[HALF:, :LANES] - block[:HALF, LANES:]


def stacked(x):
    return jnp.concatenate(eight_tiles(x, left32(x)), axis=0)


def statistics(stat_ref, sum_ref, fine_ref):
    base = stacked(stat_ref[0])
    total = stacked(stat_ref[1])
    squares = stacked(stat_ref[2])
    mean_base = mxu(jnp.concatenate(split3(base), axis=1), sum_ref[...]) * (1.0 / W)
    level = total + float(W) * (base - mean_base)
    energy = squares + level * level * (1.0 / W)
    both = jnp.concatenate([level, energy], axis=0)
    sums = mxu(jnp.concatenate(split3(both), axis=1), sum_ref[...])
    count = level.shape[0]
    mean_level = sums[:count] * (1.0 / W)
    variance = (sums[count:] - mean_level * mean_level) * (1.0 / (W * W))
    scale = lax.rsqrt(jnp.maximum(variance, 0.0) + EPS)
    hi, mid, low = split3(level - mean_level)
    wave = mxu(jnp.concatenate([hi, mid, low, hi, mid, hi], axis=1), fine_ref[...])
    lane = lax.broadcasted_iota(jnp.int32, (count, LANES), 1)
    inside = lax.rem(lane, W) != 0
    real = jnp.where(inside, wave[:, :LANES], 0.0)
    imaginary = jnp.where(inside, -wave[:, LANES:], 0.0)
    return real, imaginary, scale


def frequency32(x_ref):
    down_count, tiles = x_ref.shape[0], x_ref.shape[1]
    minus = jnp.concatenate([x_ref[i, k, 0:1, :] for k in range(tiles) for i in range(down_count)], axis=0)
    real = jnp.concatenate([x_ref[i, k, HALF : HALF + 1, :] for k in range(tiles) for i in range(down_count)], axis=0)
    return real, -minus


def cross(a_real, a_imaginary, b_real, b_imaginary):
    return (
        a_real * b_real + a_imaginary * b_imaginary,
        a_real * b_imaginary - a_imaginary * b_real,
    )


def across_back(blocks, across_ref):
    rows = []
    for block in blocks:
        hi, lo = split2(block)
        rows.append(jnp.concatenate([hi, lo, hi], axis=1))
    return mxu(jnp.concatenate(rows, axis=0), across_ref[...])


def edges(x_ref, stat_ref, sum_ref, fine_ref, edge_ref):
    real, imaginary, scale = statistics(stat_ref, sum_ref, fine_ref)
    last_real, last_imaginary = frequency32(x_ref)
    for n, value in enumerate((real, imaginary, last_real, last_imaginary, scale)):
        edge_ref[n] = value


def edge_rows(a, b, across_ref, row_ref):
    scale = a[4] * b[4] * (1.0 / (W * W * W))
    p = cross(a[0], a[1], b[0], b[1])
    r = cross(a[2], a[3], b[2], b[3])
    back = across_back([*p, *r], across_ref)
    n = scale.shape[0]
    row_ref[0] = (back[:n, :LANES] - back[n : 2 * n, LANES:]) * scale
    row_ref[1] = (back[2 * n : 3 * n, :LANES] - back[3 * n :, LANES:]) * scale
    row_ref[2] = scale


def halfway(i, first_ref, second_ref, across_ref, row_ref, half_ref):
    down_count, tiles = first_ref.shape[0], first_ref.shape[1]
    left = lax.broadcasted_iota(jnp.int32, (W, LANES), 1) < W
    slot0 = lax.broadcasted_iota(jnp.int32, (HALF, LANES), 0) == 0
    blocks = []
    for k in range(tiles):
        a_real, a_imaginary = first_ref[i, k, 0:HALF, :], first_ref[i, k, HALF:W, :]
        b_real, b_imaginary = second_ref[i, k, 0:HALF, :], second_ref[i, k, HALF:W, :]
        blocks.append(jnp.concatenate(cross(a_real, a_imaginary, b_real, b_imaginary), axis=0))
    back = across_back(blocks, across_ref)
    lines = []
    for k in range(tiles):
        block = back[W * k : W * (k + 1)]
        at = down_count * k + i
        scale = row_ref[2, at : at + 1, :]
        real = (block[:HALF, :LANES] - block[HALF:, LANES:]) * scale
        imaginary = (block[HALF:, :LANES] + block[:HALF, LANES:]) * scale
        real = jnp.where(slot0, row_ref[0, at : at + 1, :], real)
        imaginary = jnp.where(slot0, row_ref[1, at : at + 1, :], imaginary)
        lines.append(jnp.concatenate([real, imaginary], axis=0))
    for t in range(tiles // 2):
        even, odd = lines[t], lines[tiles // 2 + t]
        for n, pair in enumerate(
            (jnp.where(left, even, pltpu.roll(odd, W, 1)), jnp.where(left, pltpu.roll(even, W, 1), odd))
        ):
            hi, lo = split2(pair)
            lanes = slice(LANES * (2 * t + n), LANES * (2 * t + n + 1))
            half_ref[i, 0:W, lanes] = hi
            half_ref[i, W : 2 * W, lanes] = lo


def finish(i, half_ref, up_ref, plane_ref):
    hi = half_ref[i, 0:W, :]
    plane_ref[i] = mxu(up_ref[...], jnp.concatenate([hi, half_ref[i, W : 2 * W, :], hi], axis=0))


def packed_columns(x):
    rows = x.shape[0] // 4
    lane = lax.broadcasted_iota(jnp.int32, (rows, LANES), 1)
    out = x[:rows]
    for q in range(1, 4):
        out = jnp.where(lane < STRIDE * q, out, pltpu.roll(x[rows * q : rows * (q + 1)], STRIDE * q, 1))
    return out


def strips_kernel(tile_ref, next_ref, row_ref, col_ref, slab_ref, sems):
    slabs, rows = [], []
    for n, ref in enumerate((tile_ref, next_ref)):
        slabs.append(pltpu.make_async_copy(ref.at[:, pl.ds(0, LANES)], slab_ref.at[n], sems.at[n]))
        rows.append(pltpu.make_async_copy(ref.at[pl.ds(0, STRIDE), :], row_ref.at[n], sems.at[2 + n]))
    for copy in slabs + rows:
        copy.start()
    for n, copy in enumerate(slabs):
        copy.wait()
        col_ref[n] = packed_columns(slab_ref[n])
    for copy in rows:
        copy.wait()


def strips(tile, following):
    height, breadth = following.shape
    return pl.pallas_call(
        strips_kernel,
        out_shape=(
            jax.ShapeDtypeStruct((2, STRIDE, breadth), F32),
            jax.ShapeDtypeStruct((2, height // 4, LANES), F32),
        ),
        in_specs=[ANY, ANY],
        out_specs=(VMEM, VMEM),
        scratch_shapes=[pltpu.VMEM((2, height, LANES), F32), pltpu.SemaphoreType.DMA((4,))],
        compiler_params=pltpu.CompilerParams(vmem_limit_bytes=STRIPS_VMEM),
        name="strips",
    )(*(pltpu.with_memory_space_constraint(x, pltpu.HBM) for x in (tile, following)))


def load_kernel(*refs):
    count = len(refs) // 2
    sems = refs[-1]
    copies = [pltpu.make_async_copy(refs[n], refs[count + n], sems.at[n]) for n in range(count)]
    for copy in copies:
        copy.start()
    for copy in copies:
        copy.wait()


def load(*arrays):
    return pl.pallas_call(
        load_kernel,
        out_shape=tuple(jax.ShapeDtypeStruct(x.shape, x.dtype) for x in arrays),
        in_specs=[ANY] * len(arrays),
        out_specs=(VMEM,) * len(arrays),
        scratch_shapes=[pltpu.SemaphoreType.DMA((len(arrays),))],
        compiler_params=pltpu.CompilerParams(vmem_limit_bytes=STRIPS_VMEM),
        name="load",
    )(*(pltpu.with_memory_space_constraint(x, pltpu.HBM) for x in arrays))


def corners_kernel(col_ref, out_ref):
    for n in range(out_ref.shape[0]):
        out_ref[n] = packed_columns(col_ref[n, :STRIDE, :])


def corners(cols):
    return pl.pallas_call(
        corners_kernel,
        out_shape=jax.ShapeDtypeStruct((cols.shape[0], STRIDE // 4, LANES), F32),
        in_specs=[VMEM],
        out_specs=VMEM,
        compiler_params=pltpu.CompilerParams(vmem_limit_bytes=SMALL_VMEM),
        name="corners",
    )(cols)


def joined_kernel(row_ref, col_ref, corner_ref, out_ref):
    tall = row_ref.shape[2] // LANES * STRIDE
    for t in range(tall // STRIDE):
        out_ref[STRIDE * t : STRIDE * (t + 1), :] = row_ref[0, :, LANES * t : LANES * (t + 1)]
    out_ref[tall : tall + col_ref.shape[1], :] = col_ref[0]
    out_ref[tall + col_ref.shape[1] :, :] = corner_ref[0]


def joined(rows, cols, corner):
    tall = rows.shape[2] // LANES * STRIDE
    return pl.pallas_call(
        joined_kernel,
        out_shape=jax.ShapeDtypeStruct((tall + cols.shape[1] + corner.shape[1], LANES), F32),
        in_specs=[VMEM] * 3,
        out_specs=VMEM,
        compiler_params=pltpu.CompilerParams(vmem_limit_bytes=SMALL_VMEM),
        name="joined",
    )(rows, cols, corner)


def rims_of(row, cols, corner, row_last, col_last):
    return (
        jnp.where(row_last, 0.0, row),
        jnp.where(col_last, 0.0, cols),
        jnp.where(jnp.logical_or(row_last, col_last), 0.0, corner),
    )


def first_kernel(
    place, tile_ref, row_ref, col_ref, corner_ref, table_ref, x_ref, edge_ref, stat_ref
):
    row_last, col_last, _ = place()
    down_ref, across_ref, fine_ref, _, sum_ref = table_refs(table_ref)
    rims = rims_of(row_ref[0], col_ref[0], corner_ref[0], row_last, col_last)
    forward(tile_ref[...], rims, down_ref, across_ref, x_ref, stat_ref)
    edges(x_ref, stat_ref, sum_ref, fine_ref, edge_ref)


def second_kernel(
    place, tile_ref, following_ref, rim_ref, row_ref, col_ref, corner_ref, first_ref, first_edge,
    table_ref,
    out_ref,
    second_ref, stat_ref, second_edge, line_ref, half_ref, plane_ref, sems,
):
    row_last, col_last, last = place()
    down_ref, across_ref, fine_ref, up_ref, sum_ref = table_refs(table_ref)
    tile = jnp.where(last, following_ref[...], tile_ref[...])
    tall = tile.shape[1] // LANES * STRIDE
    wide = tall + col_ref.shape[1]
    row = jnp.concatenate([rim_ref[STRIDE * t : STRIDE * (t + 1), :] for t in range(tall // STRIDE)], axis=1)
    row = jnp.where(last, row_ref[1], row)
    cols = jnp.where(last, col_ref[1], rim_ref[tall:wide, :])
    corner = jnp.where(last, corner_ref[1], rim_ref[wide:, :])
    rims = rims_of(row, cols, corner, row_last, col_last)
    forward(tile, rims, down_ref, across_ref, second_ref, stat_ref)
    edges(second_ref, stat_ref, sum_ref, fine_ref, second_edge)
    edge_rows(first_edge, second_edge, across_ref, line_ref)
    down_count = first_ref.shape[0]
    copies = []
    for i in range(down_count):
        halfway(i, first_ref, second_ref, across_ref, line_ref, half_ref)
        if i >= LAG:
            finish(i - LAG, half_ref, up_ref, plane_ref)
        if i >= LAG and (i - LAG) % GROUP == GROUP - 1:
            copies.append(send(plane_ref, out_ref, sems, i - LAG))
    for i in range(down_count - LAG, down_count):
        finish(i, half_ref, up_ref, plane_ref)
        if i % GROUP == GROUP - 1:
            copies.append(send(plane_ref, out_ref, sems, i))
    for copy in copies:
        copy.wait()


def send(plane_ref, out_ref, sems, i):
    rows = pl.ds(i + 1 - GROUP, GROUP)
    copy = pltpu.make_async_copy(plane_ref.at[rows], out_ref.at[0, rows], sems.at[i])
    copy.start()
    return copy


def sizes(height, breadth):
    down_count = height // STRIDE
    tiles = 2 * breadth // LANES
    return down_count, tiles, (down_count, tiles, W, LANES), (3, down_count, breadth + LANES)


def first(place, tile, rows, cols, corner, table):
    down_count, tiles, spectrum, stat = sizes(*tile.shape)
    return pl.pallas_call(
        functools.partial(first_kernel, place),
        out_shape=tuple(jax.ShapeDtypeStruct(shape, F32) for shape in (spectrum, (5, tiles * down_count, LANES))),
        in_specs=[VMEM] * 5,
        out_specs=(VMEM,) * 2,
        scratch_shapes=[pltpu.VMEM(stat, F32)],
        compiler_params=pltpu.CompilerParams(vmem_limit_bytes=FIRST_VMEM),
        cost_estimate=pl.CostEstimate(flops=3 * 10**9, bytes_accessed=3 << 20, transcendentals=0),
        name="first",
    )(tile, rows, cols, corner, table)


def second(place, tile, following, rims, rows, cols, corner, spectrum, edge, table):
    height, breadth = tile.shape
    down_count, tiles, shape, stat_shape = sizes(height, breadth)
    return pl.pallas_call(
        functools.partial(second_kernel, place),
        out_shape=jax.ShapeDtypeStruct((1, down_count, W, 2 * breadth), F32),
        in_specs=[VMEM] * 9,
        out_specs=ANY,
        scratch_shapes=[
            pltpu.VMEM(shape, F32),
            pltpu.VMEM(stat_shape, F32),
            pltpu.VMEM((5, tiles * down_count, LANES), F32),
            pltpu.VMEM((3, tiles * down_count, LANES), F32),
            pltpu.VMEM((down_count, 2 * W, 2 * breadth), BF16),
            pltpu.VMEM((down_count, W, 2 * breadth), F32),
            pltpu.SemaphoreType.DMA((down_count,)),
        ],
        compiler_params=pltpu.CompilerParams(vmem_limit_bytes=SECOND_VMEM),
        cost_estimate=pl.CostEstimate(flops=8 * 10**9, bytes_accessed=5 << 20, transcendentals=0),
        name="second",
    )(tile, following, rims, rows, cols, corner, spectrum, edge, table)


def turned_down(x, axis):
    devices = lax.axis_size(axis)
    return lax.ppermute(x, axis, [(i, (i - 1) % devices) for i in range(devices)])


def moved_down(x, axis):
    return lax.ppermute(x, axis, [(i, i - 1) for i in range(1, lax.axis_size(axis))])


def place():
    return tuple(lax.axis_index(axis) == lax.axis_size(axis) - 1 for axis in ("row", "col", "tm"))


def on_device(frames, following):
    tile = frames[0]
    rows, cols = strips(tile, following)
    cols = turned_down(cols, "col")
    arriving = turned_down(tile, "tm")
    rows = turned_down(rows, "row")
    tile, following, table = load(tile, following, jnp.asarray(make_tables(), BF16))
    corner = turned_down(corners(cols), "row")
    rims = moved_down(joined(rows, cols, corner), "tm")
    spectrum, edge = first(place, tile, rows, cols, corner, table)
    return second(place, arriving, following, rims, rows, cols, corner, spectrum, edge, table)


def solution(mesh):
    in_specs = (P("tm", "row", "col"), P("row", "col"))
    out_specs = P("tm", "row", None, "col")


    return jax.shard_map(on_device, mesh=mesh, in_specs=in_specs, out_specs=out_specs, check_vma=False)
```

```python
import functools

import jax
import jax.numpy as jnp
import ml_dtypes
import numpy as np
from jax import lax
from jax.experimental import pallas as pl
from jax.experimental.pallas import tpu as pltpu
from jax.sharding import PartitionSpec as P


W = 64
STRIDE = 32
HALF = W // 2
LANES = 128
EPS = 1e-05
F32 = jnp.float32
BF16 = jnp.bfloat16
LAG = 5
BATCH = 2
BACK = 1
ANY = pl.BlockSpec(memory_space=pl.ANY)
VMEM = pl.BlockSpec(memory_space=pltpu.VMEM)
STRIPS_VMEM = 4 << 20
SMALL_VMEM = 2 << 20
FIRST_VMEM = 8 << 20
SECOND_VMEM = 16 << 20


def parts_of(table, count):
    rest = np.asarray(table, np.float64)
    out = []
    for _ in range(count):
        part = rest.astype(ml_dtypes.bfloat16)
        out.append(part)
        rest = rest - part.astype(np.float64)
    return out


def two_windows(block):
    zero = np.zeros_like(block)
    return np.block([[block, zero], [zero, block]])


def make_tables():
    index = np.arange(W)
    turns = 2.0 * np.pi / W * (index[:, None] * index[None, :] % W)
    cosine, sine = np.cos(turns), np.sin(turns)
    down = np.concatenate([cosine[:HALF], -sine[:HALF]], axis=0)
    down[0] = 0.0
    down[HALF] = cosine[HALF]
    hi, lo = parts_of(down, 2)
    down_table = np.concatenate([hi, hi, lo], axis=1)
    across = np.concatenate([two_windows(cosine), two_windows(sine)], axis=1)
    hi, lo, low = parts_of(across, 3)
    across_table = np.concatenate([hi, hi, lo], axis=0)
    fine_table = np.concatenate([hi, hi, hi, lo, lo, low], axis=0)
    up = np.concatenate([2.0 * cosine[:, :HALF], -2.0 * sine[:, :HALF]], axis=1)
    up[:, 0] = 1.0
    up[:, HALF] = cosine[HALF]
    hi, lo = parts_of(up, 2)
    up_table = np.concatenate([hi, hi, lo], axis=1)
    ones = two_windows(np.ones((W, W))).astype(ml_dtypes.bfloat16)
    sum_table = np.concatenate([ones, ones, ones], axis=0)
    tables = (down_table, across_table, fine_table, up_table, sum_table)
    return np.concatenate([np.pad(t, ((0, 0), (0, TABLE_LANES - t.shape[1]))) for t in tables], axis=0)


TABLES = ((W, 3 * W), (3 * LANES, 2 * LANES), (6 * LANES, 2 * LANES), (W, 3 * W), (3 * LANES, LANES))
TABLE_LANES = 2 * LANES


def table_refs(ref):
    out, at = [], 0
    for rows, lanes in TABLES:
        out.append(ref.at[at : at + rows, 0:lanes])
        at += rows
    return out


def mxu(a, b):
    return jnp.dot(a, b, preferred_element_type=F32)


def split2(x):
    hi = x.astype(BF16)
    lo = (x - hi.astype(F32)).astype(BF16)
    return hi, lo


def split3(x):
    hi = x.astype(BF16)
    rest = x - hi.astype(F32)
    mid = rest.astype(BF16)
    low = (rest - mid.astype(F32)).astype(BF16)
    return hi, mid, low


def left32(x):
    return pltpu.roll(x, x.shape[1] - STRIDE, 1)


def eight_tiles(x, shifted):
    count = x.shape[1] // LANES - 1
    return [x[:, LANES * t : LANES * (t + 1)] for t in range(count)] + [
        shifted[:, LANES * t : LANES * (t + 1)] for t in range(count)
    ]


def column_block(pack, corner, b):
    blocks = 2 * LANES // STRIDE
    if b == blocks:
        return jnp.concatenate([quarter(corner, q) for q in range(LANES // STRIDE)], axis=0)
    return quarter(pack[STRIDE * (b % 2) : STRIDE * (b % 2) + STRIDE], b // 2)


def quarter(x, q):
    return pltpu.roll(x, LANES - STRIDE * q, 1) if q else x


def column_rim(rims, i):
    _, pack, corner = rims
    return jnp.concatenate([column_block(pack, corner, i), column_block(pack, corner, i + 1)], axis=0)


def window_rows(tile, row, i):
    top = STRIDE * i
    if top + W <= tile.shape[0]:
        return tile[top : top + W]
    return jnp.concatenate([tile[top:], row], axis=0)


def down(pixels, down_ref):
    base = pixels[0:1, :]
    above = pixels - base
    total = jnp.sum(above, axis=0, keepdims=True)
    centred = above - total * (1.0 / W)
    squares = jnp.sum(centred * centred, axis=0, keepdims=True)
    hi, lo = split2(centred)
    return mxu(down_ref[...], jnp.concatenate([hi, lo, hi], axis=0)), (base, total, squares)


def across(tiles, across_ref, targets):
    spectrum = across_back(tiles, across_ref)
    for k, target in enumerate(targets):
        block = spectrum[W * k : W * (k + 1)]
        target[0:HALF, :] = block[:HALF, :LANES] + block[HALF:, LANES:]
        target[HALF:W, :] = block[HALF:, :LANES] - block[:HALF, LANES:]


def note(stat_ref, i, lanes, values):
    for n, value in enumerate(values):
        stat_ref[n, i : i + 1, lanes] = value


def forward(tile, rims, down_ref, across_ref, x_ref, stat_ref):
    tiles, targets = [], []
    for i in range(x_ref.shape[0]):
        pixels = jnp.concatenate([window_rows(tile, rims[0], i), column_rim(rims, i)], axis=1)
        columns, stats = down(pixels, down_ref)
        note(stat_ref, i, slice(0, pixels.shape[1]), stats)
        tiles += eight_tiles(columns, left32(columns))
        targets += [x_ref.at[i, k] for k in range(x_ref.shape[1])]
        if (i + 1) % BATCH == 0:
            across(tiles, across_ref, targets)
            tiles, targets = [], []


def stacked(x):
    return jnp.concatenate(eight_tiles(x, left32(x)), axis=0)


def statistics(stat_ref, sum_ref, fine_ref):
    base = stacked(stat_ref[0])
    total = stacked(stat_ref[1])
    squares = stacked(stat_ref[2])
    mean_base = mxu(jnp.concatenate(split3(base), axis=1), sum_ref[...]) * (1.0 / W)
    level = total + float(W) * (base - mean_base)
    energy = squares + level * level * (1.0 / W)
    both = jnp.concatenate([level, energy], axis=0)
    sums = mxu(jnp.concatenate(split3(both), axis=1), sum_ref[...])
    count = level.shape[0]
    mean_level = sums[:count] * (1.0 / W)
    variance = (sums[count:] - mean_level * mean_level) * (1.0 / (W * W))
    scale = lax.rsqrt(jnp.maximum(variance, 0.0) + EPS)
    hi, mid, low = split3(level - mean_level)
    wave = mxu(jnp.concatenate([hi, mid, low, hi, mid, hi], axis=1), fine_ref[...])
    lane = lax.broadcasted_iota(jnp.int32, (count, LANES), 1)
    inside = lax.rem(lane, W) != 0
    real = jnp.where(inside, wave[:, :LANES], 0.0)
    imaginary = jnp.where(inside, -wave[:, LANES:], 0.0)
    return real, imaginary, scale


def frequency32(x_ref):
    down_count, tiles = x_ref.shape[:2]
    minus = jnp.concatenate([x_ref[i, k, 0:1, :] for k in range(tiles) for i in range(down_count)], axis=0)
    real = jnp.concatenate([x_ref[i, k, HALF : HALF + 1, :] for k in range(tiles) for i in range(down_count)], axis=0)
    return real, -minus


def cross(a_real, a_imaginary, b_real, b_imaginary):
    return (
        a_real * b_real + a_imaginary * b_imaginary,
        a_real * b_imaginary - a_imaginary * b_real,
    )


def across_back(blocks, across_ref):
    rows = []
    for block in blocks:
        hi, lo = split2(block)
        rows.append(jnp.concatenate([hi, lo, hi], axis=1))
    return mxu(jnp.concatenate(rows, axis=0), across_ref[...])


def edges(x_ref, stat_ref, sum_ref, fine_ref, edge_ref):
    real, imaginary, scale = statistics(stat_ref, sum_ref, fine_ref)
    last_real, last_imaginary = frequency32(x_ref)
    for n, value in enumerate((real, imaginary, last_real, last_imaginary, scale)):
        edge_ref[n] = value


def edge_rows(a, b, across_ref, row_ref):
    scale = a[4] * b[4] * (1.0 / (W * W * W))
    p = cross(a[0], a[1], b[0], b[1])
    r = cross(a[2], a[3], b[2], b[3])
    back = across_back([*p, *r], across_ref)
    n = scale.shape[0]
    row_ref[0] = (back[:n, :LANES] - back[n : 2 * n, LANES:]) * scale
    row_ref[1] = (back[2 * n : 3 * n, :LANES] - back[3 * n :, LANES:]) * scale
    row_ref[2] = scale


def halfway(windows, first_ref, second_ref, across_ref, row_ref, half_ref):
    down_count, tiles = first_ref.shape[0], first_ref.shape[1]
    blocks = []
    for i in windows:
        for k in range(tiles):
            a_real, a_imaginary = first_ref[i, k, 0:HALF, :], first_ref[i, k, HALF:W, :]
            b_real, b_imaginary = second_ref[i, k, 0:HALF, :], second_ref[i, k, HALF:W, :]
            blocks.append(jnp.concatenate(cross(a_real, a_imaginary, b_real, b_imaginary), axis=0))
    back = across_back(blocks, across_ref)
    for n, i in enumerate(windows):
        settle(i, back[W * tiles * n : W * tiles * (n + 1)], down_count, tiles, row_ref, half_ref)


def settle(i, back, down_count, tiles, row_ref, half_ref):
    left = lax.broadcasted_iota(jnp.int32, (W, LANES), 1) < W
    slot0 = lax.broadcasted_iota(jnp.int32, (HALF, LANES), 0) == 0
    lines = []
    for k in range(tiles):
        block = back[W * k : W * (k + 1)]
        at = down_count * k + i
        scale = row_ref[2, at : at + 1, :]
        real = (block[:HALF, :LANES] - block[HALF:, LANES:]) * scale
        imaginary = (block[HALF:, :LANES] + block[:HALF, LANES:]) * scale
        real = jnp.where(slot0, row_ref[0, at : at + 1, :], real)
        imaginary = jnp.where(slot0, row_ref[1, at : at + 1, :], imaginary)
        lines.append(jnp.concatenate([real, imaginary], axis=0))
    for t in range(tiles // 2):
        even, odd = lines[t], lines[tiles // 2 + t]
        for n, pair in enumerate(
            (jnp.where(left, even, pltpu.roll(odd, W, 1)), jnp.where(left, pltpu.roll(even, W, 1), odd))
        ):
            hi, lo = split2(pair)
            lanes = slice(LANES * (2 * t + n), LANES * (2 * t + n + 1))
            half_ref[i, 0:W, lanes] = hi
            half_ref[i, W : 2 * W, lanes] = lo


def finish(i, half_ref, up_ref, plane_ref):
    hi = half_ref[i, 0:W, :]
    plane_ref[i] = mxu(up_ref[...], jnp.concatenate([hi, half_ref[i, W : 2 * W, :], hi], axis=0))


def packed_columns(x):
    rows = x.shape[0] // 4
    lane = lax.broadcasted_iota(jnp.int32, (rows, LANES), 1)
    out = x[:rows]
    for q in range(1, 4):
        out = jnp.where(lane < STRIDE * q, out, pltpu.roll(x[rows * q : rows * (q + 1)], STRIDE * q, 1))
    return out


def strips_kernel(tile_ref, next_ref, row_ref, col_ref, slab_ref, sems):
    slabs, rows = [], []
    for n, ref in enumerate((tile_ref, next_ref)):
        slabs.append(pltpu.make_async_copy(ref.at[:, pl.ds(0, LANES)], slab_ref.at[n], sems.at[n]))
        rows.append(pltpu.make_async_copy(ref.at[pl.ds(0, STRIDE), :], row_ref.at[n], sems.at[2 + n]))
    for copy in slabs + rows:
        copy.start()
    for n, copy in enumerate(slabs):
        copy.wait()
        col_ref[n] = packed_columns(slab_ref[n])
    for copy in rows:
        copy.wait()


def strips(tile, following):
    height, breadth = following.shape
    return pl.pallas_call(
        strips_kernel,
        out_shape=(
            jax.ShapeDtypeStruct((2, STRIDE, breadth), F32),
            jax.ShapeDtypeStruct((2, height // 4, LANES), F32),
        ),
        in_specs=[ANY, ANY],
        out_specs=(VMEM, VMEM),
        scratch_shapes=[pltpu.VMEM((2, height, LANES), F32), pltpu.SemaphoreType.DMA((4,))],
        compiler_params=pltpu.CompilerParams(vmem_limit_bytes=STRIPS_VMEM),
        name="strips",
    )(*(pltpu.with_memory_space_constraint(x, pltpu.HBM) for x in (tile, following)))


def load_kernel(*refs):
    count = len(refs) // 2
    sems = refs[-1]
    copies = [pltpu.make_async_copy(refs[n], refs[count + n], sems.at[n]) for n in range(count)]
    for copy in copies:
        copy.start()
    for copy in copies:
        copy.wait()


def load(*arrays):
    return pl.pallas_call(
        load_kernel,
        out_shape=tuple(jax.ShapeDtypeStruct(x.shape, x.dtype) for x in arrays),
        in_specs=[ANY] * len(arrays),
        out_specs=(VMEM,) * len(arrays),
        scratch_shapes=[pltpu.SemaphoreType.DMA((len(arrays),))],
        compiler_params=pltpu.CompilerParams(vmem_limit_bytes=STRIPS_VMEM),
        name="load",
    )(*(pltpu.with_memory_space_constraint(x, pltpu.HBM) for x in arrays))


def corners_kernel(col_ref, out_ref):
    for n in range(out_ref.shape[0]):
        out_ref[n] = packed_columns(col_ref[n, :STRIDE, :])


def corners(cols):
    return pl.pallas_call(
        corners_kernel,
        out_shape=jax.ShapeDtypeStruct((cols.shape[0], STRIDE // 4, LANES), F32),
        in_specs=[VMEM],
        out_specs=VMEM,
        compiler_params=pltpu.CompilerParams(vmem_limit_bytes=SMALL_VMEM),
        name="corners",
    )(cols)


def joined_kernel(row_ref, col_ref, corner_ref, out_ref):
    tall = row_ref.shape[2] // LANES * STRIDE
    for t in range(tall // STRIDE):
        out_ref[STRIDE * t : STRIDE * (t + 1), :] = row_ref[0, :, LANES * t : LANES * (t + 1)]
    out_ref[tall : tall + col_ref.shape[1], :] = col_ref[0]
    out_ref[tall + col_ref.shape[1] :, :] = corner_ref[0]


def joined(rows, cols, corner):
    tall = rows.shape[2] // LANES * STRIDE
    return pl.pallas_call(
        joined_kernel,
        out_shape=jax.ShapeDtypeStruct((tall + cols.shape[1] + corner.shape[1], LANES), F32),
        in_specs=[VMEM] * 3,
        out_specs=VMEM,
        compiler_params=pltpu.CompilerParams(vmem_limit_bytes=SMALL_VMEM),
        name="joined",
    )(rows, cols, corner)


def rims_of(row, cols, corner, row_last, col_last):
    return (
        jnp.where(row_last, 0.0, row),
        jnp.where(col_last, 0.0, cols),
        jnp.where(jnp.logical_or(row_last, col_last), 0.0, corner),
    )


def first_kernel(
    place, tile_ref, row_ref, col_ref, corner_ref, table_ref, x_ref, edge_ref, stat_ref
):
    row_last, col_last, _ = place()
    down_ref, across_ref, fine_ref, _, sum_ref = table_refs(table_ref)
    rims = rims_of(row_ref[0], col_ref[0], corner_ref[0], row_last, col_last)
    forward(tile_ref[...], rims, down_ref, across_ref, x_ref, stat_ref)
    edges(x_ref, stat_ref, sum_ref, fine_ref, edge_ref)


def second_kernel(
    place, tile_ref, following_ref, rim_ref, row_ref, col_ref, corner_ref, first_ref, first_edge,
    table_ref,
    out_ref,
    second_ref, stat_ref, second_edge, line_ref, half_ref, plane_ref, sems,
):
    row_last, col_last, last = place()
    down_ref, across_ref, fine_ref, up_ref, sum_ref = table_refs(table_ref)
    down_count, _ = first_ref.shape[:2]
    tile = jnp.where(last, following_ref[...], tile_ref[...])
    tall = tile.shape[1] // LANES * STRIDE
    wide = tall + col_ref.shape[1]
    row = jnp.concatenate([rim_ref[STRIDE * t : STRIDE * (t + 1), :] for t in range(tall // STRIDE)], axis=1)
    row = jnp.where(last, row_ref[1], row)
    cols = jnp.where(last, col_ref[1], rim_ref[tall:wide, :])
    corner = jnp.where(last, corner_ref[1], rim_ref[wide:, :])
    rims = rims_of(row, cols, corner, row_last, col_last)
    forward(tile, rims, down_ref, across_ref, second_ref, stat_ref)
    edges(second_ref, stat_ref, sum_ref, fine_ref, second_edge)
    edge_rows(first_edge, second_edge, across_ref, line_ref)
    copies, done = [], 0

    def complete(until):
        for i in range(done, until):
            finish(i, half_ref, up_ref, plane_ref)
            copies.append(send(plane_ref, out_ref, sems, i))
        return max(done, until)

    for i in range(0, down_count, BACK):
        halfway(range(i, i + BACK), first_ref, second_ref, across_ref, line_ref, half_ref)
        done = complete(i + BACK - LAG)
    complete(down_count)
    for copy in copies:
        copy.wait()


def send(plane_ref, out_ref, sems, i):
    copy = pltpu.make_async_copy(plane_ref.at[i], out_ref.at[0, i], sems.at[i])
    copy.start()
    return copy


def sizes(height, breadth):
    down_count = height // STRIDE
    tiles = 2 * breadth // LANES
    return down_count, tiles, (down_count, tiles, W, LANES), (3, down_count, breadth + LANES)


def first(place, tile, rows, cols, corner, table):
    down_count, tiles, spectrum, stat = sizes(*tile.shape)
    return pl.pallas_call(
        functools.partial(first_kernel, place),
        out_shape=tuple(jax.ShapeDtypeStruct(shape, F32) for shape in (spectrum, (5, tiles * down_count, LANES))),
        in_specs=[VMEM] * 5,
        out_specs=(VMEM,) * 2,
        scratch_shapes=[pltpu.VMEM(stat, F32)],
        compiler_params=pltpu.CompilerParams(vmem_limit_bytes=FIRST_VMEM),
        cost_estimate=pl.CostEstimate(flops=3 * 10**9, bytes_accessed=3 << 20, transcendentals=0),
        name="first",
    )(tile, rows, cols, corner, table)


def second(place, tile, following, rims, rows, cols, corner, spectrum, edge, table):
    height, breadth = tile.shape
    down_count, tiles, shape, stat_shape = sizes(height, breadth)
    return pl.pallas_call(
        functools.partial(second_kernel, place),
        out_shape=jax.ShapeDtypeStruct((1, down_count, W, 2 * breadth), F32),
        in_specs=[VMEM] * 9,
        out_specs=ANY,
        scratch_shapes=[
            pltpu.VMEM(shape, F32),
            pltpu.VMEM(stat_shape, F32),
            pltpu.VMEM((5, tiles * down_count, LANES), F32),
            pltpu.VMEM((3, tiles * down_count, LANES), F32),
            pltpu.VMEM((down_count, 2 * W, 2 * breadth), BF16),
            pltpu.VMEM((down_count, W, 2 * breadth), F32),
            pltpu.SemaphoreType.DMA((down_count,)),
        ],
        compiler_params=pltpu.CompilerParams(vmem_limit_bytes=SECOND_VMEM),
        cost_estimate=pl.CostEstimate(flops=8 * 10**9, bytes_accessed=5 << 20, transcendentals=0),
        name="second",
    )(
        tile, following, rims, rows, cols, corner, spectrum, edge, table
    )


def turned_down(x, axis):
    devices = lax.axis_size(axis)
    return lax.ppermute(x, axis, [(i, (i - 1) % devices) for i in range(devices)])


def moved_down(x, axis):
    return lax.ppermute(x, axis, [(i, i - 1) for i in range(1, lax.axis_size(axis))])


def place():
    return tuple(lax.axis_index(axis) == lax.axis_size(axis) - 1 for axis in ("row", "col", "tm"))


def on_device(frames, following):
    tile = frames[0]
    rows, cols = strips(tile, following)
    cols = turned_down(cols, "col")
    arriving = turned_down(tile, "tm")
    rows = turned_down(rows, "row")
    tile, following, table = load(tile, following, jnp.asarray(make_tables(), BF16))
    corner = turned_down(corners(cols), "row")
    rims = moved_down(joined(rows, cols, corner), "tm")
    spectrum, edge = first(place, tile, rows, cols, corner, table)
    return second(place, arriving, following, rims, rows, cols, corner, spectrum, edge, table)


def solution(mesh):
    in_specs = (P("tm", "row", "col"), P("row", "col"))
    out_specs = P("tm", "row", None, "col")


    return jax.shard_map(on_device, mesh=mesh, in_specs=in_specs, out_specs=out_specs, check_vma=False)
```
